32 devices in a mesh: dp: 4 (over z), fsdp: 8 (over y, x, core).
Axes of the slice: x: 2, y: 2, z: 4, core: 2. Of those that a mesh axis runs over, the one named last changes fastest.
Arguments:
- embed_table: bfloat16 [8192, 128], P(('dp', 'fsdp')), may hold values from -43 to 43
- token_ids: int32 [16384], P(('dp', 'fsdp')), may hold values from 0 to 8191
- time_steps: int32 [16384], P(('dp', 'fsdp')), may hold values from 0 to 1999, as said below
- segment_ids: int32 [16384], P(('dp', 'fsdp')), may hold values from 0 to 7, as said below
- noise_draw: bfloat16 [16384, 128], P(('dp', 'fsdp')), may hold values from -6 to 6
- w_up: bfloat16 [128, 768], P(None, ('dp', 'fsdp')), may hold values from -0.5 to 0.5
- w_time: bfloat16 [128, 768], P(None, ('dp', 'fsdp')), may hold values from -0.5 to 0.5
- w_qkv: bfloat16 [768, 2304], P(None, ('dp', 'fsdp')), may hold values from -0.21875 to 0.21875
- w_out: bfloat16 [768, 768], P(None, ('dp', 'fsdp')), may hold values from -0.875 to 0.875
- w_in: bfloat16 [768, 3072], P(None, ('dp', 'fsdp')), may hold values from -0.21875 to 0.21875
- w_down: bfloat16 [3072, 768], P(('dp', 'fsdp')), may hold values from -0.109375 to 0.109375
- gain_one: bfloat16 [768], P(('dp', 'fsdp')), may hold values from 0.099609375 to 1.8984375
- gain_two: bfloat16 [768], P(('dp', 'fsdp')), may hold values from 0.099609375 to 1.8984375
- cotangent: bfloat16 [16384, 768], P(('dp', 'fsdp')), may hold values from -6 to 6
Outputs:
- output: bfloat16 [16384, 768], P(('dp', 'fsdp'))
- table_grad: float32 [8192, 128], P(('dp', 'fsdp'))
- noise_grad: float32 [16384, 128], P(('dp', 'fsdp'))
- up_grad: float32 [128, 768], P(None, ('dp', 'fsdp'))
- time_grad: float32 [128, 768], P(None, ('dp', 'fsdp'))
- qkv_grad: float32 [768, 2304], P(None, ('dp', 'fsdp'))
- out_grad: float32 [768, 768], P(None, ('dp', 'fsdp'))
- in_grad: float32 [768, 3072], P(None, ('dp', 'fsdp'))
- down_grad: float32 [3072, 768], P(('dp', 'fsdp'))
- gain_one_grad: float32 [768], P(('dp', 'fsdp'))
- gain_two_grad: float32 [768], P(('dp', 'fsdp'))
The draws below stay inside these ranges and needn't reach their ends.
Inputs may be any that keep to these rules, and one draw needn't show every extreme that they name: `segment_ids`: the tokens of each device are whole items: in every aligned block of 512 tokens the ids are either all 0 (one item) or count items of 64 tokens from 0 in order; both kinds of block occur in every draw. `time_steps`: all tokens of one item have the same time step.
All inputs are finite; a program needn't handle non-finite values.
Results may differ from the reference program's by a relative error of at most 0.014.
Values may be sent and summed in bfloat16 or wider, within the bound.
A program may use at most 128 MiB of HBM per device.

```python
import math
import jax
import jax.numpy as jnp
import numpy as np
from jax import lax

D = 768
HEADS = 12
HEAD_DIM = 64
FF = 3072
EMBED = 128
VOCAB = 8192
TIME_DIM = 128
STEPS = 2000
SHORT_LEN = 64
TOK_DEV = 512
TOKENS = 16384


def item_layout(key):
    device_blocks = TOKENS // TOK_DEV
    per_block = TOK_DEV // SHORT_LEN
    long_flags = jax.random.randint(jax.random.fold_in(key, 7), (device_blocks,), 0, 2)
    long_flags = long_flags.at[0].set(0).at[1].set(1)
    local_ids = jnp.arange(TOK_DEV, dtype=jnp.int32) // SHORT_LEN
    seg_table = jnp.where(long_flags[:, None] == 1, 0, local_ids[None, :]).astype(jnp.int32)
    item_steps = jax.random.randint(jax.random.fold_in(key, 13), (device_blocks, per_block), 0, STEPS)
    item_steps = item_steps.at[0, 0].set(0).at[0, 1].set(STEPS - 1)
    token_steps = jnp.take_along_axis(item_steps, seg_table, axis=1)
    return (seg_table.reshape(TOKENS).astype(jnp.int32), token_steps.reshape(TOKENS).astype(jnp.int32))


def draw_segment_ids(key, part):
    return item_layout(jax.random.fold_in(key, 101))[0]


def draw_time_steps(key, part):
    return item_layout(jax.random.fold_in(key, 101))[1]


def draw_embed_table(key, part):
    first_key, second_key, third_key = jax.random.split(key, 3)
    rising = jnp.exp(math.log(3.0) * jnp.arange(VOCAB, dtype=jnp.float32) / VOCAB)
    row_scale = rising * jnp.exp(jax.random.uniform(first_key, (VOCAB,), minval=0.0, maxval=math.log(10.0)))
    col_scale = jnp.exp(jax.random.uniform(second_key, (EMBED,), minval=0.0, maxval=math.log(4.0)))
    base_values = jnp.clip(jax.random.normal(third_key, (VOCAB, EMBED)), -4.0, 4.0)
    values = base_values * row_scale[:, None] * col_scale[None, :] / math.sqrt(128.0)
    return values.astype(jnp.bfloat16)


def with_ends(array, stream_key, smallest, high):
    longest = array.shape.index(max(array.shape))
    spots = []
    for shift in (0, 1):
        where = [jax.random.randint(jax.random.fold_in(stream_key, axis), (), 0, length) for axis, length in enumerate(array.shape)]
        where[longest] = (where[longest] + shift) % array.shape[longest]
        spots.append(tuple(where))
    return array.at[spots[0]].set(smallest).at[spots[1]].set(high)


def levels(stream_key, dims, pieces, least, high):
    level, own = 1.0, jax.random.fold_in(stream_key, 6)
    for axis_at, parts in pieces:
        steps = jnp.exp(jax.random.uniform(jax.random.fold_in(own, axis_at), (parts,), jnp.float32, least / len(pieces), high / len(pieces)))
        level = level * jnp.repeat(steps, dims[axis_at] // parts).reshape([-1 if axis == axis_at else 1 for axis in range(len(dims))])
    return level


def rank_bounds(amount, slope):
    portions = [(1 << 20) // math.isqrt(grade ** slope) + 1 for grade in range(1, amount + 1)]
    width = 1 + sum(portions) // (1 << 30)
    return np.cumsum(np.array([max(1, weight // width) for weight in portions]))


def ranked(own_key, shape, count, slope):
    table = rank_bounds(count, slope)
    pick = jax.random.randint(jax.random.fold_in(own_key, 1), shape, 0, int(table[count - 1]))
    standing = jnp.searchsorted(jnp.asarray(table, jnp.int32), pick, side="right")
    return jax.random.permutation(jax.random.fold_in(own_key, 2), count)[standing].astype(jnp.int32)


def centred(stream_key, shape, width, most, cuts=(), kind=jnp.bfloat16):
    loudness = levels(stream_key, shape, cuts, -0.22, 0.18) if cuts else 1.0
    array = jax.random.normal(stream_key, shape, jnp.float32) * width * loudness
    return jnp.minimum(jnp.maximum(array, -most), most).astype(kind)


def setup_inputs(seed: int = 0) -> dict:
    arg_keys = jax.random.split(jax.random.key(seed), 15)
    return {
        "embed_table": draw_embed_table(jax.random.fold_in(arg_keys[14], 71), 0),
        "token_ids": with_ends(ranked(arg_keys[1], (TOKENS,), VOCAB, 2), jax.random.fold_in(arg_keys[1], 3), 0, VOCAB - 1).astype(jnp.int32),
        "time_steps": draw_time_steps(jax.random.fold_in(arg_keys[14], 71), 0),
        "segment_ids": draw_segment_ids(jax.random.fold_in(arg_keys[14], 71), 0),
        "noise_draw": centred(arg_keys[4], (TOKENS, EMBED), 1.0, 6.0, ((0, 32),)),
        "w_up": centred(arg_keys[5], (EMBED, D), EMBED ** -0.5, 0.5, ((1, 32),)),
        "w_time": centred(arg_keys[6], (TIME_DIM, D), TIME_DIM ** -0.5, 0.5, ((1, 32),)),
        "w_qkv": centred(arg_keys[7], (D, 3 * D), D ** -0.5, 0.21875, ((1, 32),)),
        "w_out": centred(arg_keys[8], (D, D), (D // 16) ** -0.5, 0.875, ((1, 32),)),
        "w_in": centred(arg_keys[9], (D, FF), D ** -0.5, 0.21875, ((1, 32),)),
        "w_down": centred(arg_keys[10], (FF, D), FF ** -0.5, 0.109375, ((0, 32),)),
        "gain_one": jnp.clip(1.0 + 0.18 * jax.random.normal(arg_keys[11], (D,), jnp.float32), 0.099609375, 1.8984375).astype(jnp.bfloat16),
        "gain_two": jnp.clip(1.0 + 0.18 * jax.random.normal(arg_keys[12], (D,), jnp.float32), 0.099609375, 1.8984375).astype(jnp.bfloat16),
        "cotangent": centred(arg_keys[13], (TOKENS, D), 1.0, 6.0, ((0, 32),)),
    }


@jax.custom_vjp
def low(v):
    return lax.optimization_barrier(v.astype(jnp.bfloat16)).astype(jnp.float32)

@jax.custom_vjp
def low_back(v):
    return v

def low_keep(v):
    return (low(v), None)

def low_pass(kept, grad):
    return (grad,)

def back_keep(v):
    return (v, None)

def back_low(kept, grad):
    return (low(grad),)
low.defvjp(low_keep, low_pass)
low_back.defvjp(back_keep, back_low)

def matmul(left, right):
    return jnp.dot(left, right, precision=lax.Precision.HIGHEST, preferred_element_type=jnp.float32)

def layer_norm(values, gain):
    center = values - lax.optimization_barrier(jnp.mean(values, axis=1, keepdims=True))
    spread = lax.optimization_barrier(jnp.mean(center * center, axis=1, keepdims=True))
    return center * lax.rsqrt(spread + 1e-05) * gain

def time_features(time_steps):
    half_dim = TIME_DIM // 2
    frequency = jnp.exp(-math.log(10000.0) * jnp.arange(half_dim, dtype=jnp.float32) / half_dim)
    angles = time_steps.astype(jnp.float32)[:, None] * frequency[None, :]
    return jnp.concatenate([jnp.sin(angles), jnp.cos(angles)], axis=1)

def attend_device(operands):
    query_part, key_part, value_part, seg_part = operands
    q_heads = query_part.reshape(TOK_DEV, HEADS, HEAD_DIM)
    k_heads = key_part.reshape(TOK_DEV, HEADS, HEAD_DIM)
    v_heads = value_part.reshape(TOK_DEV, HEADS, HEAD_DIM)
    scores = jnp.einsum('qhd,khd->hqk', q_heads, k_heads, precision=lax.Precision.HIGHEST) * (1.0 / math.sqrt(HEAD_DIM))
    scores = low_back(scores)
    allowed = seg_part[:, None] == seg_part[None, :]
    scores = jnp.where(allowed[None], scores, -1e+30)
    row_peak = lax.optimization_barrier(jnp.max(scores, axis=2, keepdims=True))
    weights = jnp.exp(scores - row_peak)
    soft_probs = low(weights / lax.optimization_barrier(jnp.sum(weights, axis=2, keepdims=True)))
    context = jnp.einsum('hqk,khd->qhd', soft_probs, v_heads, precision=lax.Precision.HIGHEST)
    return context.reshape(TOK_DEV, HEADS * HEAD_DIM)

def reference(embed_table, token_ids, time_steps, segment_ids, noise_draw, w_up, w_time, w_qkv, w_out, w_in, w_down, gain_one, gain_two, cotangent):
    level_value = time_steps.astype(jnp.float32) / STEPS + 0.0001
    signal = jnp.sqrt(1.0 - jnp.sqrt(level_value))
    blur_level = jnp.sqrt(jnp.sqrt(level_value))
    time_feats = low(time_features(time_steps))
    device_count = TOKENS // TOK_DEV
    table_plain = embed_table.astype(jnp.float32)
    norm_values = jnp.sqrt(lax.optimization_barrier(jnp.sum(table_plain * table_plain, axis=1)) + 1e-06)
    factor = math.sqrt(EMBED) / jnp.mean(norm_values)

    def forward(table_f, noise_f, up_f, time_f, qkv_f, out_f, in_f, down_f, gain_one_f, gain_two_f):
        picked = jnp.take(table_f, token_ids, axis=0) * factor
        noisy_input = low(signal[:, None] * picked + blur_level[:, None] * noise_f)
        embedded = low_back(matmul(noisy_input, up_f) + matmul(time_feats, time_f))
        normed = low(layer_norm(embedded, gain_one_f))
        mixed_qkv = matmul(normed, qkv_f)
        query_part = low(low_back(mixed_qkv[:, :D]))
        key_part = low(low_back(mixed_qkv[:, D:2 * D]))
        value_part = low(low_back(mixed_qkv[:, 2 * D:]))
        context = lax.map(jax.checkpoint(attend_device), (query_part.reshape(device_count, TOK_DEV, D), key_part.reshape(device_count, TOK_DEV, D), value_part.reshape(device_count, TOK_DEV, D), segment_ids.reshape(device_count, TOK_DEV)))
        context = low(low_back(context.reshape(TOKENS, D)))
        branch = low_back(matmul(context, out_f))
        middle = embedded + branch
        normed_two = low(layer_norm(middle, gain_two_f))
        pre_act = low_back(matmul(normed_two, in_f))
        activated = low(jax.nn.gelu(pre_act, approximate=False))
        return middle + low_back(matmul(activated, down_f))
    floats = tuple((array_in.astype(jnp.float32) for array_in in (embed_table, noise_draw, w_up, w_time, w_qkv, w_out, w_in, w_down, gain_one, gain_two)))
    result, pullback = jax.vjp(forward, *floats)
    grads = pullback(cotangent.astype(jnp.float32))
    return (result.astype(jnp.bfloat16), grads[0], grads[1], grads[2], grads[3], grads[4], grads[5], grads[6], grads[7], grads[8], grads[9])
```

```python
import functools
import math

import jax
import jax.numpy as jnp
from jax import lax
from jax.experimental import pallas as pl
from jax.experimental.pallas import tpu as pltpu
from jax.sharding import PartitionSpec as P

HEADS = 12
HEAD_DIM = 64
EMBED = 128
VOCAB = 8192
TIME_DIM = 128
STEPS = 2000


def layer_norm(values, gain):
    center = values - jnp.mean(values, axis=1, keepdims=True)
    spread = jnp.mean(center * center, axis=1, keepdims=True)
    return center * lax.rsqrt(spread + 1e-05) * gain


def matmul(left, right):
    return jnp.dot(left, right, preferred_element_type=jnp.float32)


def matmul_left(left, right):
    return lax.dot_general(
        left, right, (((0,), (0,)), ((), ())), preferred_element_type=jnp.float32
    )


def matmul_right(left, right):
    return lax.dot_general(
        left, right, (((1,), (1,)), ((), ())), preferred_element_type=jnp.float32
    )


def gelu_exact(values):
    return jax.nn.gelu(values, approximate=False)


def time_features(time_steps):
    half_dim = TIME_DIM // 2
    frequency = jnp.exp(-math.log(10000.0) * jnp.arange(half_dim, dtype=jnp.float32) / half_dim)
    angles = time_steps.astype(jnp.float32)[:, None] * frequency[None, :]
    return jnp.concatenate([jnp.sin(angles), jnp.cos(angles)], axis=1)


def block_scores(q_block, k_heads, seg_block, seg_whole):
    scores = jnp.einsum("qhd,khd->hqk", q_block, k_heads, preferred_element_type=jnp.float32) * (
        1.0 / math.sqrt(HEAD_DIM)
    )
    allowed = seg_block[:, None] == seg_whole[None, :]
    return jnp.where(allowed[None], scores, -1e30)


def attention_forward(query_part, key_part, value_part, segments):
    row_count = query_part.shape[0]
    q_heads = query_part.reshape(row_count, HEADS, HEAD_DIM)
    k_heads = key_part.reshape(row_count, HEADS, HEAD_DIM)
    v_heads = value_part.reshape(row_count, HEADS, HEAD_DIM)
    scores = block_scores(q_heads, k_heads, segments, segments)
    row_peak = jnp.max(scores, axis=2, keepdims=True)
    weights = jnp.exp(scores - row_peak)
    row_total = jnp.sum(weights, axis=2, keepdims=True)
    soft_probs = (weights / row_total).astype(jnp.bfloat16)
    contexts = jnp.einsum("hqk,khd->qhd", soft_probs, v_heads, preferred_element_type=jnp.float32)
    log_totals = row_peak + jnp.log(row_total)
    context = contexts.reshape(row_count, HEADS * HEAD_DIM).astype(jnp.bfloat16)
    return (context, log_totals)


def attention_backward(query_part, key_part, value_part, segments, log_total, grad_context):
    row_count = query_part.shape[0]
    score_scale = 1.0 / math.sqrt(HEAD_DIM)
    q_heads = query_part.reshape(row_count, HEADS, HEAD_DIM)
    k_heads = key_part.reshape(row_count, HEADS, HEAD_DIM)
    v_heads = value_part.reshape(row_count, HEADS, HEAD_DIM)
    g_heads = grad_context.reshape(row_count, HEADS, HEAD_DIM)
    scores = block_scores(q_heads, k_heads, segments, segments)
    soft_probs = jnp.exp(scores - log_total)
    probs_low = soft_probs.astype(jnp.bfloat16)
    grad_probs = jnp.einsum("qhd,khd->hqk", g_heads, v_heads, preferred_element_type=jnp.float32)
    grad_value = jnp.einsum("hqk,qhd->khd", probs_low, g_heads, preferred_element_type=jnp.float32)
    grad_scores = soft_probs * (
        grad_probs - jnp.sum(soft_probs * grad_probs, axis=2, keepdims=True)
    )
    grad_scores = grad_scores.astype(jnp.bfloat16)
    query_pieces = (
        jnp.einsum("hqk,khd->qhd", grad_scores, k_heads, preferred_element_type=jnp.float32)
        * score_scale
    )
    grad_key = (
        jnp.einsum("hqk,qhd->khd", grad_scores, q_heads, preferred_element_type=jnp.float32)
        * score_scale
    )
    grad_query = query_pieces.reshape(row_count, HEADS * HEAD_DIM).astype(jnp.bfloat16)
    grad_key = grad_key.reshape(row_count, HEADS * HEAD_DIM).astype(jnp.bfloat16)
    grad_value = grad_value.reshape(row_count, HEADS * HEAD_DIM).astype(jnp.bfloat16)
    return (grad_query, grad_key, grad_value)


def native_local(
    embed_table,
    token_ids,
    time_steps,
    segment_ids,
    noise_draw,
    w_up,
    w_time,
    w_qkv,
    w_out,
    w_in,
    w_down,
    gain_one,
    gain_two,
    cotangent,
):
    table_values = embed_table.astype(jnp.float32)
    norm_values = jnp.sqrt(jnp.sum(table_values * table_values, axis=1) + 1e-06)
    norm_total = lax.psum(jnp.sum(norm_values), ("dp", "fsdp"))
    mean_norm = norm_total / VOCAB
    factor = math.sqrt(EMBED) / mean_norm
    gathered = (
        lax.all_gather(embed_table, ("dp", "fsdp"), axis=0, tiled=True),
        lax.all_gather(w_up, ("dp", "fsdp"), axis=1, tiled=True),
        lax.all_gather(w_time, ("dp", "fsdp"), axis=1, tiled=True),
        lax.all_gather(w_qkv, ("dp", "fsdp"), axis=1, tiled=True),
        lax.all_gather(w_out, ("dp", "fsdp"), axis=1, tiled=True),
        lax.all_gather(w_in, ("dp", "fsdp"), axis=1, tiled=True),
        lax.all_gather(w_down, ("dp", "fsdp"), axis=0, tiled=True),
        lax.all_gather(gain_one, ("dp", "fsdp"), axis=0, tiled=True),
        lax.all_gather(gain_two, ("dp", "fsdp"), axis=0, tiled=True),
    )
    (
        full_table,
        up_full,
        time_full,
        qkv_full,
        out_full,
        in_full,
        down_full,
        gain_first,
        gain_second,
    ) = gathered
    raw_rows = jnp.take(full_table, token_ids, axis=0).astype(jnp.float32)
    level_value = time_steps.astype(jnp.float32) / STEPS + 0.0001
    signal = jnp.sqrt(1.0 - jnp.sqrt(level_value))
    blur_level = jnp.sqrt(jnp.sqrt(level_value))
    noisy_input = (
        signal[:, None] * (raw_rows * factor) + blur_level[:, None] * noise_draw.astype(jnp.float32)
    ).astype(jnp.bfloat16)
    time_feats = time_features(time_steps).astype(jnp.bfloat16)
    embedded = matmul(noisy_input, up_full) + matmul(time_feats, time_full)
    normed = layer_norm(embedded, gain_first.astype(jnp.float32)).astype(jnp.bfloat16)
    mixed_qkv = matmul(normed, qkv_full)
    width = mixed_qkv.shape[1] // 3
    query_part = mixed_qkv[:, :width].astype(jnp.bfloat16)
    key_part = mixed_qkv[:, width : 2 * width].astype(jnp.bfloat16)
    value_part = mixed_qkv[:, 2 * width :].astype(jnp.bfloat16)
    context, log_total = attention_forward(query_part, key_part, value_part, segment_ids)
    middle = embedded + matmul(context, out_full)
    normed_two = layer_norm(middle, gain_second.astype(jnp.float32)).astype(jnp.bfloat16)
    pre_act = matmul(normed_two, in_full)
    activated = gelu_exact(pre_act).astype(jnp.bfloat16)
    output = (middle + matmul(activated, down_full)).astype(jnp.bfloat16)
    again = (
        lax.all_gather(w_up, ("dp", "fsdp"), axis=1, tiled=True),
        lax.all_gather(w_time, ("dp", "fsdp"), axis=1, tiled=True),
        lax.all_gather(w_qkv, ("dp", "fsdp"), axis=1, tiled=True),
        lax.all_gather(w_out, ("dp", "fsdp"), axis=1, tiled=True),
        lax.all_gather(w_in, ("dp", "fsdp"), axis=1, tiled=True),
        lax.all_gather(w_down, ("dp", "fsdp"), axis=0, tiled=True),
        lax.all_gather(gain_one, ("dp", "fsdp"), axis=0, tiled=True),
        lax.all_gather(gain_two, ("dp", "fsdp"), axis=0, tiled=True),
    )
    up_back, time_back, qkv_back, out_back, in_back, down_back, gain_third, gain_fourth = again
    grad_down = matmul_left(activated, cotangent)
    grad_act = matmul_right(cotangent, down_back)
    unused_gelu, gelu_pull = jax.vjp(gelu_exact, pre_act)
    grad_pre = gelu_pull(grad_act)[0].astype(jnp.bfloat16)
    grad_in = matmul_left(normed_two, grad_pre)
    grad_normed_two = matmul_right(grad_pre, in_back)
    unused_second, second_pull = jax.vjp(layer_norm, middle, gain_fourth.astype(jnp.float32))
    grad_middle_norm, grad_gain_two = second_pull(grad_normed_two)
    grad_middle = cotangent.astype(jnp.float32) + grad_middle_norm
    mlp_shards = (
        lax.psum_scatter(grad_in, ("dp", "fsdp"), scatter_dimension=1, tiled=True),
        lax.psum_scatter(grad_down, ("dp", "fsdp"), scatter_dimension=0, tiled=True),
        lax.psum_scatter(grad_gain_two, ("dp", "fsdp"), scatter_dimension=0, tiled=True),
    )
    grad_branch = grad_middle.astype(jnp.bfloat16)
    grad_out = matmul_left(context, grad_branch)
    grad_context = matmul_right(grad_branch, out_back).astype(jnp.bfloat16)
    grad_query, grad_key, grad_value = attention_backward(
        query_part, key_part, value_part, segment_ids, log_total, grad_context
    )
    grad_mixed = jnp.concatenate([grad_query, grad_key, grad_value], axis=1)
    grad_qkv = matmul_left(normed, grad_mixed)
    grad_normed = matmul_right(grad_mixed, qkv_back)
    unused_first, first_pull = jax.vjp(layer_norm, embedded, gain_third.astype(jnp.float32))
    grad_embed_norm, grad_gain_one = first_pull(grad_normed)
    grad_embedded = (grad_middle + grad_embed_norm).astype(jnp.bfloat16)
    grad_up = matmul_left(noisy_input, grad_embedded)
    grad_time = matmul_left(time_feats, grad_embedded)
    grad_noisy = matmul_right(grad_embedded, up_back)
    noise_grad = blur_level[:, None] * grad_noisy
    grad_rows = signal[:, None] * grad_noisy
    counted = jnp.zeros((VOCAB, EMBED), jnp.float32).at[token_ids].add(grad_rows)
    rest_shards = (
        lax.psum_scatter(counted, ("dp", "fsdp"), scatter_dimension=0, tiled=True),
        lax.psum_scatter(grad_up, ("dp", "fsdp"), scatter_dimension=1, tiled=True),
        lax.psum_scatter(grad_time, ("dp", "fsdp"), scatter_dimension=1, tiled=True),
        lax.psum_scatter(grad_qkv, ("dp", "fsdp"), scatter_dimension=1, tiled=True),
        lax.psum_scatter(grad_out, ("dp", "fsdp"), scatter_dimension=1, tiled=True),
        lax.psum_scatter(grad_gain_one, ("dp", "fsdp"), scatter_dimension=0, tiled=True),
    )
    counted_own, up_own, time_own, qkv_own, out_own, gain_one_own = rest_shards
    in_own, down_own, gain_two_own = mlp_shards
    table_grad = factor * counted_own
    return (
        output,
        table_grad,
        noise_grad,
        up_own,
        time_own,
        qkv_own,
        out_own,
        in_own,
        down_own,
        gain_one_own,
        gain_two_own,
    )


MESH = pl.DeviceIdType.MESH


class Grid:
    def __init__(self, Z, F):
        self.Z, self.F = Z, F
        self.X = math.isqrt(F // 2); self.Y = F // 2 // self.X
    def here(self):
        z = lax.axis_index("dp"); f = lax.axis_index("fsdp")
        return z, f // (2 * self.X), (f // 2) % self.X, f % 2
    def dev(self, z, y, x, c):
        return (z, (y * self.X + x) * 2 + c)

def barrier(g):
    z, y, x, c = g.here()
    bar = pltpu.get_barrier_semaphore()
    n = 0
    peers = [g.dev((z + k) % g.Z, y, x, c) for k in range(1, g.Z)]
    peers += [g.dev(z, (y + k) % g.Y, x, c) for k in range(1, g.Y)]
    peers += [g.dev(z, y, (x + k) % g.X, c) for k in range(1, g.X)]
    peers += [g.dev(z, y, x, 1 - c)]
    for p in peers:
        pl.semaphore_signal(bar, inc=1, device_id=p, device_id_type=MESH)
    pl.semaphore_wait(bar, len(peers))

class Gather:
    def __init__(self, g, shard, full, cut, local_sem, send, recv):
        self.g = g
        r, C = shard.shape
        self.r, self.C = r, C
        self.shard = shard
        self.full = full
        kind, at = cut
        if kind == "lane":
            self.h = ((slice(None), pl.ds(0, at)), (slice(None), pl.ds(at, C - at)))
        else:
            self.h = ((pl.ds(0, at), slice(None)), (pl.ds(at, r - at), slice(None)))
        self.local_sem, self.send, self.recv = local_sem, send, recv
        self.i = 0
        self.groups = {}
    def cp(self, name, src, dst, dev):
        c = pltpu.make_async_remote_copy(src_ref=src, dst_ref=dst, send_sem=self.send.at[self.i], recv_sem=self.recv.at[self.i], device_id=dev, device_id_type=MESH)
        self.i += 1
        c.start()
        self.groups.setdefault(name, []).append(c)
    def wait(self, name):
        for c in self.groups[name]:
            c.wait_recv()
    def finish(self):
        for cs in self.groups.values():
            for c in cs: c.wait_send()
    def s1(self):
        g = self.g; z, y, x, c = g.here()
        self.local = pltpu.make_async_copy(self.shard, self.full.at[z, y, x, c], self.local_sem)
        self.local.start()
        for k in range(1, g.Z):
            self.cp("z", self.shard, self.full.at[z, y, x, c], g.dev((z + k) % g.Z, y, x, c))
    def s2(self):
        g = self.g; z, y, x, c = g.here()
        self.local.wait()
        self.wait("z")
        a, b = self.h
        for k in range(1, g.X):
            v = self.full.at[:, y, x, c, a[0], a[1]]
            self.cp("a2", v, v, g.dev(z, y, (x + k) % g.X, c))
        for k in range(1, g.Y):
            v = self.full.at[:, y, x, c, b[0], b[1]]
            self.cp("b2", v, v, g.dev(z, (y + k) % g.Y, x, c))
        v = self.full.at[:, y, x, c]
        self.cp("sib1", v, v, g.dev(z, y, x, 1 - c))
    def s3(self):
        g = self.g; z, y, x, c = g.here()
        self.wait("a2"); self.wait("b2")
        a, b = self.h
        for k in range(1, g.Y):
            v = self.full.at[:, y, :, c, a[0], a[1]]
            self.cp("a3", v, v, g.dev(z, (y + k) % g.Y, x, c))
        for k in range(1, g.X):
            v = self.full.at[:, :, x, c, b[0], b[1]]
            self.cp("b3", v, v, g.dev(z, y, (x + k) % g.X, c))
        sib = g.dev(z, y, x, 1 - c)
        for k in range(1, g.X):
            v = self.full.at[:, y, (x + g.X - k) % g.X, c, a[0], a[1]]
            self.cp("sib2", v, v, sib)
        for k in range(1, g.Y):
            v = self.full.at[:, (y + g.Y - k) % g.Y, x, c, b[0], b[1]]
            self.cp("sib2", v, v, sib)
    def s4(self):
        g = self.g; z, y, x, c = g.here()
        self.wait("a3"); self.wait("b3")
        a, b = self.h
        sib = g.dev(z, y, x, 1 - c)
        for k in range(1, g.Y):
            v = self.full.at[:, (y + g.Y - k) % g.Y, :, c, a[0], a[1]]
            self.cp("sib3", v, v, sib)
        for k in range(1, g.X):
            v = self.full.at[:, :, (x + g.X - k) % g.X, c, b[0], b[1]]
            self.cp("sib3", v, v, sib)
    def done(self):
        self.wait("sib1"); self.wait("sib2"); self.wait("sib3")

def n_copies(g):
    return (g.Z - 1) + (g.X - 1) + (g.Y - 1) + 1 + 2 * (g.X - 1 + g.Y - 1) + (g.X - 1 + g.Y - 1)

def ag_kernel(g, cuts, *refs):
    n = len(cuts)
    shards, fulls = refs[:n], refs[n:2 * n]
    local, send, recv = refs[2 * n:]
    barrier(g)
    ts = [Gather(g, s, f, cut, local.at[i], send.at[i], recv.at[i]) for i, (s, f, cut) in enumerate(zip(shards, fulls, cuts))]
    for t in ts: t.s1()
    for tick in range(n + 3):
        for st in (1, 2, 3, 4):
            i = tick - (st - 1)
            if 0 <= i < n:
                (ts[i].s2, ts[i].s3, ts[i].s4, ts[i].done)[st - 1]()
    for t in ts: t.finish()

def gather_all(g, shards, cuts, space):
    n = len(shards)
    outs = tuple(jax.ShapeDtypeStruct((g.Z, g.Y, g.X, 2, *s.shape), s.dtype) for s in shards)
    nc = n_copies(g)
    fulls = pl.pallas_call(
        functools.partial(ag_kernel, g, cuts),
        out_shape=outs,
        in_specs=[pl.BlockSpec(memory_space=pltpu.VMEM)] * n,
        out_specs=tuple([pl.BlockSpec(memory_space=space)] * n),
        scratch_shapes=[pltpu.SemaphoreType.DMA((n,)), pltpu.SemaphoreType.DMA((n, nc)), pltpu.SemaphoreType.DMA((n, nc))],
        compiler_params=pltpu.CompilerParams(collective_id=0, has_side_effects=True, vmem_limit_bytes=60 * 2**20),
        name="gather_weights",
    )(*shards)
    return [f.reshape(g.Z * g.F * s.shape[0], s.shape[1]) for f, s in zip(fulls, shards)]


def halves(r, C, cut):
    kind, at = cut
    if kind == "lane":
        return ((pl.ds(0, r), pl.ds(0, at)), (pl.ds(0, r), pl.ds(at, C - at)))
    return ((pl.ds(0, at), pl.ds(0, C)), (pl.ds(at, r - at), pl.ds(0, C)))


def half_shapes(r, C, cut):
    kind, at = cut
    return ((r, at), (r, C - at)) if kind == "lane" else ((at, C), (r - at, C))


class Scatter:
    def __init__(self, g, part, out, cut, bufs, send, recv):
        self.g, self.out = g, out
        self.part = part
        r, C = part.shape[-2:]
        self.a, self.b = halves(r, C, cut)
        self.sib, self.r1a, self.r1b, self.r2a, self.r2b, self.r3 = bufs
        self.send, self.recv = send, recv
        self.i = 0
        self.groups = {}

    def copy(self, name, src, dst, dev):
        c = pltpu.make_async_remote_copy(
            src_ref=src, dst_ref=dst, send_sem=self.send.at[self.i], recv_sem=self.recv.at[self.i],
            device_id=dev, device_id_type=MESH,
        )
        self.i += 1
        c.start()
        self.groups.setdefault(name, []).append(c)

    def wait(self, name):
        for c in self.groups.get(name, []):
            c.wait_recv()

    def finish(self):
        for cs in self.groups.values():
            for c in cs:
                c.wait_send()

    def s0(self):
        g = self.g
        z, y, x, c = g.here()
        self.copy("sib", self.part.at[:, :, :, 1 - c], self.sib, g.dev(z, y, x, 1 - c))

    def s1(self):
        g = self.g
        z, y, x, c = g.here()
        self.wait("sib")

        def add(i, carry):
            iz, iy, ix = i // (g.Y * g.X), (i // g.X) % g.Y, i % g.X
            self.part[iz, iy, ix, c] = self.part[iz, iy, ix, c] + self.sib[iz, iy, ix]
            return carry

        lax.fori_loop(0, g.Z * g.Y * g.X, add, 0)
        a, b = self.a, self.b
        for k in range(1, g.Y):
            to = (y + k) % g.Y
            self.copy("a1", self.part.at[:, to, :, c, a[0], a[1]], self.r1a.at[k - 1], g.dev(z, to, x, c))
        for k in range(1, g.X):
            to = (x + k) % g.X
            self.copy("b1", self.part.at[:, :, to, c, b[0], b[1]], self.r1b.at[k - 1], g.dev(z, y, to, c))

    def s2(self):
        g = self.g
        z, y, x, c = g.here()
        self.wait("a1")
        self.wait("b1")
        a, b = self.a, self.b

        def add_a(i, carry):
            iz, ix = i // g.X, i % g.X
            v = self.part[iz, y, ix, c, a[0], a[1]].astype(jnp.float32)
            for k in range(g.Y - 1):
                v = v + self.r1a[k, iz, ix].astype(jnp.float32)
            self.part[iz, y, ix, c, a[0], a[1]] = v.astype(jnp.bfloat16)
            return carry

        lax.fori_loop(0, g.Z * g.X, add_a, 0)
        for k in range(1, g.X):
            to = (x + k) % g.X
            self.copy("a2", self.part.at[:, y, to, c, a[0], a[1]], self.r2a.at[k - 1], g.dev(z, y, to, c))

        def add_b(i, carry):
            iz, iy = i // g.Y, i % g.Y
            v = self.part[iz, iy, x, c, b[0], b[1]].astype(jnp.float32)
            for k in range(g.X - 1):
                v = v + self.r1b[k, iz, iy].astype(jnp.float32)
            self.part[iz, iy, x, c, b[0], b[1]] = v.astype(jnp.bfloat16)
            return carry

        lax.fori_loop(0, g.Z * g.Y, add_b, 0)
        for k in range(1, g.Y):
            to = (y + k) % g.Y
            self.copy("b2", self.part.at[:, to, x, c, b[0], b[1]], self.r2b.at[k - 1], g.dev(z, to, x, c))

    def s3(self):
        g = self.g
        z, y, x, c = g.here()
        self.wait("a2")
        self.wait("b2")

        def add(iz, carry):
            for h, buf, n in ((self.a, self.r2a, g.X - 1), (self.b, self.r2b, g.Y - 1)):
                v = self.part[iz, y, x, c, h[0], h[1]].astype(jnp.float32)
                for k in range(n):
                    v = v + buf[k, iz].astype(jnp.float32)
                self.part[iz, y, x, c, h[0], h[1]] = v.astype(jnp.bfloat16)
            return carry

        lax.fori_loop(0, g.Z, add, 0)
        for k in range(1, g.Z):
            to = (z + k) % g.Z
            self.copy("z", self.part.at[to, y, x, c], self.r3.at[k - 1], g.dev(to, y, x, c))

    def s4(self):
        g = self.g
        z, y, x, c = g.here()
        self.wait("z")
        v = self.part[z, y, x, c].astype(jnp.float32)
        for k in range(g.Z - 1):
            v = v + self.r3[k].astype(jnp.float32)
        self.out[...] = v


def scatter_buffers(g, N, C, cut):
    r = N // (g.Z * g.F)
    ha, hb = half_shapes(r, C, cut)
    return [
        pltpu.VMEM((g.Z, g.Y, g.X, r, C), jnp.bfloat16),
        pltpu.VMEM((g.Y - 1, g.Z, g.X, *ha), jnp.bfloat16),
        pltpu.VMEM((g.X - 1, g.Z, g.Y, *hb), jnp.bfloat16),
        pltpu.VMEM((g.X - 1, g.Z, *ha), jnp.bfloat16),
        pltpu.VMEM((g.Y - 1, g.Z, *hb), jnp.bfloat16),
        pltpu.VMEM((g.Z - 1, r, C), jnp.bfloat16),
    ]


def scatter_kernel(g, cuts, *refs):
    n = len(cuts)
    parts, outs = refs[:n], refs[n : 2 * n]
    bufs = refs[2 * n : 2 * n + 6 * n]
    send, recv = refs[2 * n + 6 * n :]
    barrier(g)
    ts = [
        Scatter(g, parts[i], outs[i], cuts[i], bufs[6 * i : 6 * i + 6], send.at[i], recv.at[i])
        for i in range(n)
    ]
    for t in ts:
        t.s0()
    for tick in range(n + 3):
        for stage in range(4):
            i = tick - stage
            if 0 <= i < n:
                (ts[i].s1, ts[i].s2, ts[i].s3, ts[i].s4)[stage]()
    for t in ts:
        t.finish()


def scatter_all(g, parts, cuts):
    n = len(parts)
    outs = tuple(jax.ShapeDtypeStruct((p.shape[0] // (g.Z * g.F), p.shape[1]), jnp.float32) for p in parts)
    count = 1 + 2 * (g.X - 1 + g.Y - 1) + g.Z - 1
    bufs = []
    for p, cut in zip(parts, cuts):
        bufs += scatter_buffers(g, p.shape[0], p.shape[1], cut)
    return pl.pallas_call(
        functools.partial(scatter_kernel, g, cuts),
        out_shape=outs,
        in_specs=[pl.BlockSpec(memory_space=pltpu.VMEM)] * n,
        out_specs=tuple([pl.BlockSpec(memory_space=pltpu.VMEM)] * n),
        scratch_shapes=bufs + [pltpu.SemaphoreType.DMA((n, count)), pltpu.SemaphoreType.DMA((n, count))],
        compiler_params=pltpu.CompilerParams(
            collective_id=1, has_side_effects=True, vmem_limit_bytes=60 * 2**20
        ),
        name="scatter_gradients",
    )(*[p.reshape(g.Z, g.Y, g.X, 2, p.shape[0] // (g.Z * g.F), p.shape[1]) for p in parts])


GATHER_CUTS = [("row", 8), ("row", 128), ("lane", 256), ("lane", 384), ("lane", 384), ("lane", 384), ("lane", 384)]
SCATTER_CUTS = [("lane", 384), ("lane", 384), ("lane", 384), ("lane", 384), ("lane", 256), ("row", 128)]


def ring_local(
    g,
    embed_table,
    token_ids,
    time_steps,
    segment_ids,
    noise_draw,
    w_up,
    w_time,
    w_qkv,
    w_out,
    w_in,
    w_down,
    gain_one,
    gain_two,
    cotangent,
):
    bf = jnp.bfloat16
    table_values = embed_table.astype(jnp.float32)
    norm_values = jnp.sqrt(jnp.sum(table_values * table_values, axis=1) + 1e-06)
    norm_part = jnp.broadcast_to(jnp.sum(norm_values), (16, 128))
    rows = w_up.shape[1]
    gains = jnp.stack([gain_one, gain_two], axis=1)
    gains = jnp.concatenate([gains, jnp.zeros((rows, EMBED - 2), bf)], axis=1)
    small = jnp.concatenate([w_up.T, w_time.T, gains], axis=1)
    shards = (norm_part, embed_table, small, w_qkv.T, w_out.T, w_in.T, w_down)
    norms, full_table, small_full, qkv_t, out_t, in_t, down_full = gather_all(g, shards, GATHER_CUTS, pl.ANY)
    norm_total = jnp.sum(norms[::16, 0])
    factor = math.sqrt(EMBED) / (norm_total / VOCAB)
    embed_t = small_full[:, : 2 * EMBED]
    gain_first = small_full[:, 2 * EMBED].astype(jnp.float32)
    gain_second = small_full[:, 2 * EMBED + 1].astype(jnp.float32)

    raw_rows = jnp.take(full_table, token_ids, axis=0).astype(jnp.float32)
    level_value = time_steps.astype(jnp.float32) / STEPS + 0.0001
    signal = jnp.sqrt(1.0 - jnp.sqrt(level_value))
    blur_level = jnp.sqrt(jnp.sqrt(level_value))
    noisy_input = (
        signal[:, None] * (raw_rows * factor) + blur_level[:, None] * noise_draw.astype(jnp.float32)
    ).astype(bf)
    time_feats = time_features(time_steps).astype(bf)
    features = jnp.concatenate([noisy_input, time_feats], axis=1)
    embedded = matmul_right(features, embed_t)
    normed = layer_norm(embedded, gain_first).astype(bf)
    mixed_qkv = matmul_right(normed, qkv_t)
    width = mixed_qkv.shape[1] // 3
    query_part = mixed_qkv[:, :width].astype(bf)
    key_part = mixed_qkv[:, width : 2 * width].astype(bf)
    value_part = mixed_qkv[:, 2 * width :].astype(bf)
    context, log_total = attention_forward(query_part, key_part, value_part, segment_ids)
    middle = embedded + matmul_right(context, out_t)
    normed_two = layer_norm(middle, gain_second).astype(bf)
    pre_act = matmul_right(normed_two, in_t)
    activated = gelu_exact(pre_act).astype(bf)
    output = (middle + matmul(activated, down_full)).astype(bf)

    grad_down = matmul_left(activated, cotangent).astype(bf)
    grad_act = matmul_right(cotangent, down_full)
    unused_gelu, gelu_pull = jax.vjp(gelu_exact, pre_act)
    grad_pre = gelu_pull(grad_act)[0].astype(bf)
    grad_in = matmul_left(grad_pre, normed_two).astype(bf)
    grad_normed_two = matmul(grad_pre, in_t)
    unused_second, second_pull = jax.vjp(layer_norm, middle, gain_second)
    grad_middle_norm, grad_gain_two = second_pull(grad_normed_two)
    grad_middle = cotangent.astype(jnp.float32) + grad_middle_norm
    grad_branch = grad_middle.astype(bf)
    grad_out = matmul_left(grad_branch, context).astype(bf)
    grad_context = matmul(grad_branch, out_t).astype(bf)
    grad_query, grad_key, grad_value = attention_backward(
        query_part, key_part, value_part, segment_ids, log_total, grad_context
    )
    grad_mixed = jnp.concatenate([grad_query, grad_key, grad_value], axis=1)
    grad_qkv = matmul_left(grad_mixed, normed).astype(bf)
    grad_normed = matmul(grad_mixed, qkv_t)
    unused_first, first_pull = jax.vjp(layer_norm, embedded, gain_first)
    grad_embed_norm, grad_gain_one = first_pull(grad_normed)
    grad_embedded = (grad_middle + grad_embed_norm).astype(bf)
    grad_embed_t = matmul_left(grad_embedded, features)
    grad_noisy = matmul(grad_embedded, embed_t[:, :EMBED])
    noise_grad = blur_level[:, None] * grad_noisy
    grad_rows = signal[:, None] * grad_noisy
    counted = jnp.zeros((VOCAB, EMBED), jnp.float32).at[token_ids].add(grad_rows).astype(bf)
    grad_gains = jnp.stack([grad_gain_one, grad_gain_two], axis=1)
    grad_gains = jnp.concatenate([grad_gains, jnp.zeros((grad_gains.shape[0], EMBED - 2), jnp.float32)], axis=1)
    grad_small = jnp.concatenate([grad_embed_t, grad_gains], axis=1).astype(bf)
    down_own, in_own, out_own, qkv_own, small_own, counted_own = scatter_all(
        g, (grad_down, grad_in, grad_out, grad_qkv, grad_small, counted), SCATTER_CUTS
    )
    return (
        output,
        factor * counted_own,
        noise_grad,
        small_own[:, :EMBED].T,
        small_own[:, EMBED : 2 * EMBED].T,
        qkv_own.T,
        out_own.T,
        in_own.T,
        down_own,
        small_own[:, 2 * EMBED],
        small_own[:, 2 * EMBED + 1],
    )


def solution(mesh):
    in_specs = (
        P(("dp", "fsdp"), None),
        P(("dp", "fsdp")),
        P(("dp", "fsdp")),
        P(("dp", "fsdp")),
        P(("dp", "fsdp"), None),
        P(None, ("dp", "fsdp")),
        P(None, ("dp", "fsdp")),
        P(None, ("dp", "fsdp")),
        P(None, ("dp", "fsdp")),
        P(None, ("dp", "fsdp")),
        P(("dp", "fsdp"), None),
        P(("dp", "fsdp")),
        P(("dp", "fsdp")),
        P(("dp", "fsdp"), None),
    )
    out_specs = (
        P(("dp", "fsdp"), None),
        P(("dp", "fsdp"), None),
        P(("dp", "fsdp"), None),
        P(None, ("dp", "fsdp")),
        P(None, ("dp", "fsdp")),
        P(None, ("dp", "fsdp")),
        P(None, ("dp", "fsdp")),
        P(None, ("dp", "fsdp")),
        P(("dp", "fsdp"), None),
        P(("dp", "fsdp")),
        P(("dp", "fsdp")),
    )
    grid = Grid(mesh.shape["dp"], mesh.shape["fsdp"])

    def local(*args):
        if all(rows % 8 == 0 for rows in (args[5].shape[1], args[10].shape[0])):
            return ring_local(grid, *args)
        return native_local(*args)

    return jax.shard_map(local, mesh=mesh, in_specs=in_specs, out_specs=out_specs, check_vma=False)
```

```python
import functools
import math

import jax
import jax.numpy as jnp
from jax import lax
from jax.experimental import pallas as pl
from jax.experimental.pallas import tpu as pltpu
from jax.sharding import PartitionSpec as P

HEADS = 12
HEAD_DIM = 64
EMBED = 128
VOCAB = 8192
TIME_DIM = 128
STEPS = 2000


def layer_norm(values, gain):
    center = values - jnp.mean(values, axis=1, keepdims=True)
    spread = jnp.mean(center * center, axis=1, keepdims=True)
    return center * lax.rsqrt(spread + 1e-05) * gain


def matmul(left, right):
    return jnp.dot(left, right, preferred_element_type=jnp.float32)


def matmul_left(left, right):
    return lax.dot_general(
        left, right, (((0,), (0,)), ((), ())), preferred_element_type=jnp.float32
    )


def matmul_right(left, right):
    return lax.dot_general(
        left, right, (((1,), (1,)), ((), ())), preferred_element_type=jnp.float32
    )


def gelu_exact(values):
    return jax.nn.gelu(values, approximate=False)


def time_features(time_steps):
    half_dim = TIME_DIM // 2
    frequency = jnp.exp(-math.log(10000.0) * jnp.arange(half_dim, dtype=jnp.float32) / half_dim)
    angles = time_steps.astype(jnp.float32)[:, None] * frequency[None, :]
    return jnp.concatenate([jnp.sin(angles), jnp.cos(angles)], axis=1)


def block_scores(q_block, k_heads, seg_block, seg_whole):
    scores = jnp.einsum("qhd,khd->hqk", q_block, k_heads, preferred_element_type=jnp.float32) * (
        1.0 / math.sqrt(HEAD_DIM)
    )
    allowed = seg_block[:, None] == seg_whole[None, :]
    return jnp.where(allowed[None], scores, -1e30)


def attention_forward(query_part, key_part, value_part, segments):
    row_count = query_part.shape[0]
    q_heads = query_part.reshape(row_count, HEADS, HEAD_DIM)
    k_heads = key_part.reshape(row_count, HEADS, HEAD_DIM)
    v_heads = value_part.reshape(row_count, HEADS, HEAD_DIM)
    scores = block_scores(q_heads, k_heads, segments, segments)
    row_peak = jnp.max(scores, axis=2, keepdims=True)
    weights = jnp.exp(scores - row_peak)
    row_total = jnp.sum(weights, axis=2, keepdims=True)
    soft_probs = (weights / row_total).astype(jnp.bfloat16)
    contexts = jnp.einsum("hqk,khd->qhd", soft_probs, v_heads, preferred_element_type=jnp.float32)
    log_totals = row_peak + jnp.log(row_total)
    context = contexts.reshape(row_count, HEADS * HEAD_DIM).astype(jnp.bfloat16)
    return (context, log_totals)


def attention_backward(query_part, key_part, value_part, segments, log_total, grad_context):
    row_count = query_part.shape[0]
    score_scale = 1.0 / math.sqrt(HEAD_DIM)
    q_heads = query_part.reshape(row_count, HEADS, HEAD_DIM)
    k_heads = key_part.reshape(row_count, HEADS, HEAD_DIM)
    v_heads = value_part.reshape(row_count, HEADS, HEAD_DIM)
    g_heads = grad_context.reshape(row_count, HEADS, HEAD_DIM)
    scores = block_scores(q_heads, k_heads, segments, segments)
    soft_probs = jnp.exp(scores - log_total)
    probs_low = soft_probs.astype(jnp.bfloat16)
    grad_probs = jnp.einsum("qhd,khd->hqk", g_heads, v_heads, preferred_element_type=jnp.float32)
    grad_value = jnp.einsum("hqk,qhd->khd", probs_low, g_heads, preferred_element_type=jnp.float32)
    grad_scores = soft_probs * (
        grad_probs - jnp.sum(soft_probs * grad_probs, axis=2, keepdims=True)
    )
    grad_scores = grad_scores.astype(jnp.bfloat16)
    query_pieces = (
        jnp.einsum("hqk,khd->qhd", grad_scores, k_heads, preferred_element_type=jnp.float32)
        * score_scale
    )
    grad_key = (
        jnp.einsum("hqk,qhd->khd", grad_scores, q_heads, preferred_element_type=jnp.float32)
        * score_scale
    )
    grad_query = query_pieces.reshape(row_count, HEADS * HEAD_DIM).astype(jnp.bfloat16)
    grad_key = grad_key.reshape(row_count, HEADS * HEAD_DIM).astype(jnp.bfloat16)
    grad_value = grad_value.reshape(row_count, HEADS * HEAD_DIM).astype(jnp.bfloat16)
    return (grad_query, grad_key, grad_value)


def native_local(
    embed_table,
    token_ids,
    time_steps,
    segment_ids,
    noise_draw,
    w_up,
    w_time,
    w_qkv,
    w_out,
    w_in,
    w_down,
    gain_one,
    gain_two,
    cotangent,
):
    table_values = embed_table.astype(jnp.float32)
    norm_values = jnp.sqrt(jnp.sum(table_values * table_values, axis=1) + 1e-06)
    norm_total = lax.psum(jnp.sum(norm_values), ("dp", "fsdp"))
    mean_norm = norm_total / VOCAB
    factor = math.sqrt(EMBED) / mean_norm
    gathered = (
        lax.all_gather(embed_table, ("dp", "fsdp"), axis=0, tiled=True),
        lax.all_gather(w_up, ("dp", "fsdp"), axis=1, tiled=True),
        lax.all_gather(w_time, ("dp", "fsdp"), axis=1, tiled=True),
        lax.all_gather(w_qkv, ("dp", "fsdp"), axis=1, tiled=True),
        lax.all_gather(w_out, ("dp", "fsdp"), axis=1, tiled=True),
        lax.all_gather(w_in, ("dp", "fsdp"), axis=1, tiled=True),
        lax.all_gather(w_down, ("dp", "fsdp"), axis=0, tiled=True),
        lax.all_gather(gain_one, ("dp", "fsdp"), axis=0, tiled=True),
        lax.all_gather(gain_two, ("dp", "fsdp"), axis=0, tiled=True),
    )
    (
        full_table,
        up_full,
        time_full,
        qkv_full,
        out_full,
        in_full,
        down_full,
        gain_first,
        gain_second,
    ) = gathered
    raw_rows = jnp.take(full_table, token_ids, axis=0).astype(jnp.float32)
    level_value = time_steps.astype(jnp.float32) / STEPS + 0.0001
    signal = jnp.sqrt(1.0 - jnp.sqrt(level_value))
    blur_level = jnp.sqrt(jnp.sqrt(level_value))
    noisy_input = (
        signal[:, None] * (raw_rows * factor) + blur_level[:, None] * noise_draw.astype(jnp.float32)
    ).astype(jnp.bfloat16)
    time_feats = time_features(time_steps).astype(jnp.bfloat16)
    embedded = matmul(noisy_input, up_full) + matmul(time_feats, time_full)
    normed = layer_norm(embedded, gain_first.astype(jnp.float32)).astype(jnp.bfloat16)
    mixed_qkv = matmul(normed, qkv_full)
    width = mixed_qkv.shape[1] // 3
    query_part = mixed_qkv[:, :width].astype(jnp.bfloat16)
    key_part = mixed_qkv[:, width : 2 * width].astype(jnp.bfloat16)
    value_part = mixed_qkv[:, 2 * width :].astype(jnp.bfloat16)
    context, log_total = attention_forward(query_part, key_part, value_part, segment_ids)
    middle = embedded + matmul(context, out_full)
    normed_two = layer_norm(middle, gain_second.astype(jnp.float32)).astype(jnp.bfloat16)
    pre_act = matmul(normed_two, in_full)
    activated = gelu_exact(pre_act).astype(jnp.bfloat16)
    output = (middle + matmul(activated, down_full)).astype(jnp.bfloat16)
    again = (
        lax.all_gather(w_up, ("dp", "fsdp"), axis=1, tiled=True),
        lax.all_gather(w_time, ("dp", "fsdp"), axis=1, tiled=True),
        lax.all_gather(w_qkv, ("dp", "fsdp"), axis=1, tiled=True),
        lax.all_gather(w_out, ("dp", "fsdp"), axis=1, tiled=True),
        lax.all_gather(w_in, ("dp", "fsdp"), axis=1, tiled=True),
        lax.all_gather(w_down, ("dp", "fsdp"), axis=0, tiled=True),
        lax.all_gather(gain_one, ("dp", "fsdp"), axis=0, tiled=True),
        lax.all_gather(gain_two, ("dp", "fsdp"), axis=0, tiled=True),
    )
    up_back, time_back, qkv_back, out_back, in_back, down_back, gain_third, gain_fourth = again
    grad_down = matmul_left(activated, cotangent)
    grad_act = matmul_right(cotangent, down_back)
    unused_gelu, gelu_pull = jax.vjp(gelu_exact, pre_act)
    grad_pre = gelu_pull(grad_act)[0].astype(jnp.bfloat16)
    grad_in = matmul_left(normed_two, grad_pre)
    grad_normed_two = matmul_right(grad_pre, in_back)
    unused_second, second_pull = jax.vjp(layer_norm, middle, gain_fourth.astype(jnp.float32))
    grad_middle_norm, grad_gain_two = second_pull(grad_normed_two)
    grad_middle = cotangent.astype(jnp.float32) + grad_middle_norm
    mlp_shards = (
        lax.psum_scatter(grad_in, ("dp", "fsdp"), scatter_dimension=1, tiled=True),
        lax.psum_scatter(grad_down, ("dp", "fsdp"), scatter_dimension=0, tiled=True),
        lax.psum_scatter(grad_gain_two, ("dp", "fsdp"), scatter_dimension=0, tiled=True),
    )
    grad_branch = grad_middle.astype(jnp.bfloat16)
    grad_out = matmul_left(context, grad_branch)
    grad_context = matmul_right(grad_branch, out_back).astype(jnp.bfloat16)
    grad_query, grad_key, grad_value = attention_backward(
        query_part, key_part, value_part, segment_ids, log_total, grad_context
    )
    grad_mixed = jnp.concatenate([grad_query, grad_key, grad_value], axis=1)
    grad_qkv = matmul_left(normed, grad_mixed)
    grad_normed = matmul_right(grad_mixed, qkv_back)
    unused_first, first_pull = jax.vjp(layer_norm, embedded, gain_third.astype(jnp.float32))
    grad_embed_norm, grad_gain_one = first_pull(grad_normed)
    grad_embedded = (grad_middle + grad_embed_norm).astype(jnp.bfloat16)
    grad_up = matmul_left(noisy_input, grad_embedded)
    grad_time = matmul_left(time_feats, grad_embedded)
    grad_noisy = matmul_right(grad_embedded, up_back)
    noise_grad = blur_level[:, None] * grad_noisy
    grad_rows = signal[:, None] * grad_noisy
    counted = jnp.zeros((VOCAB, EMBED), jnp.float32).at[token_ids].add(grad_rows)
    rest_shards = (
        lax.psum_scatter(counted, ("dp", "fsdp"), scatter_dimension=0, tiled=True),
        lax.psum_scatter(grad_up, ("dp", "fsdp"), scatter_dimension=1, tiled=True),
        lax.psum_scatter(grad_time, ("dp", "fsdp"), scatter_dimension=1, tiled=True),
        lax.psum_scatter(grad_qkv, ("dp", "fsdp"), scatter_dimension=1, tiled=True),
        lax.psum_scatter(grad_out, ("dp", "fsdp"), scatter_dimension=1, tiled=True),
        lax.psum_scatter(grad_gain_one, ("dp", "fsdp"), scatter_dimension=0, tiled=True),
    )
    counted_own, up_own, time_own, qkv_own, out_own, gain_one_own = rest_shards
    in_own, down_own, gain_two_own = mlp_shards
    table_grad = factor * counted_own
    return (
        output,
        table_grad,
        noise_grad,
        up_own,
        time_own,
        qkv_own,
        out_own,
        in_own,
        down_own,
        gain_one_own,
        gain_two_own,
    )


MESH = pl.DeviceIdType.MESH


class Grid:
    def __init__(self, Z, F):
        self.Z, self.F = Z, F
        self.X = math.isqrt(F // 2)
        self.Y = F // 2 // self.X
        self.size = {"z": self.Z, "y": self.Y, "x": self.X}

    def here(self):
        f = lax.axis_index("fsdp")
        return {"z": lax.axis_index("dp"), "y": f // (2 * self.X), "x": (f // 2) % self.X, "c": f % 2}

    def dev(self, at):
        return (at["z"], (at["y"] * self.X + at["x"]) * 2 + at["c"])

    def moved(self, at, d, k):
        return {**at, d: (at[d] + k) % self.size[d]}

    def sibling(self, at):
        return {**at, "c": 1 - at["c"]}


def enter(g, at):
    bar = pltpu.get_barrier_semaphore()
    peers = [g.moved(at, d, k) for d in "zyx" for k in range(1, g.size[d])] + [g.sibling(at)]
    for p in peers:
        pl.semaphore_signal(bar, inc=1, device_id=g.dev(p), device_id_type=MESH)
    pl.semaphore_wait(bar, len(peers))


def halves(r, C, cut):
    kind, to = cut
    if kind == "lane":
        return ((pl.ds(0, r), pl.ds(0, to)), (pl.ds(0, r), pl.ds(to, C - to)))
    return ((pl.ds(0, to), pl.ds(0, C)), (pl.ds(to, r - to), pl.ds(0, C)))


def half_shapes(r, C, cut):
    kind, to = cut
    return ((r, to), (r, C - to)) if kind == "lane" else ((to, C), (r - to, C))


class Mover:
    def __init__(self, send, recv):
        self.send, self.recv, self.count, self.groups = send, recv, 0, {}

    def copy(self, group, src, dst, dev):
        c = pltpu.make_async_remote_copy(
            src_ref=src, dst_ref=dst, send_sem=self.send.at[self.count], recv_sem=self.recv.at[self.count],
            device_id=dev, device_id_type=MESH,
        )
        self.count += 1
        c.start()
        self.groups.setdefault(group, []).append(c)

    def wait(self, group):
        for c in self.groups.get(group, []):
            c.wait_recv()

    def sent(self):
        for cs in self.groups.values():
            for c in cs:
                c.wait_send()
        self.groups = {}


def gather_copies(g):
    return 2 * (sum(n - 1 for n in g.size.values()) + 1 + sum(n - 1 for n in g.size.values()))


class Gather:
    def __init__(self, g, at, mover, shard, full, cut, orders):
        self.g, self.at, self.mover, self.shard, self.full = g, at, mover, shard, full
        self.halves = halves(*shard.shape, cut)
        self.orders = orders
        self.rows = shard.shape[0]

    def view(self, h, index):
        rows, lanes = self.halves[h]
        return self.full.at[index["z"], index["y"], index["x"], self.at["c"], rows, lanes]

    def own(self, sem):
        at = self.at
        rows, lanes = self.halves[0][0], self.halves[0][1]
        self.local = pltpu.make_async_copy(
            self.shard, self.full.at[at["z"], at["y"], at["x"], at["c"], pl.ds(0, self.rows)], sem
        )
        self.local.start()

    def held(self, h, stage):
        at = self.at
        return {d: slice(None) if d in self.orders[h][:stage] else at[d] for d in "zyx"}

    def send(self, stage):
        g, at = self.g, self.at
        if stage == 2:
            self.local.wait()
        for h in (0, 1):
            d = self.orders[h][stage - 1]
            if stage > 1:
                self.mover.wait((h, stage - 1))
            for k in range(1, g.size[d]):
                dst = self.view(h, self.held(h, stage - 1))
                src = dst if stage > 1 else self.shard.at[self.halves[h]]
                self.mover.copy((h, stage), src, dst, g.dev(g.moved(at, d, k)))
        for h in (0, 1):
            if stage > 1:
                self.share(h, stage - 1)

    def share(self, h, stage):
        g, at = self.g, self.at
        d = self.orders[h][stage - 1]
        sib = g.dev(g.sibling(at))
        if stage == 1:
            v = self.view(h, self.held(h, 1))
            self.mover.copy("sib", v, v, sib)
            return
        for k in range(1, g.size[d]):
            index = {**self.held(h, stage - 1), d: g.moved(at, d, -k)[d]}
            v = self.view(h, index)
            self.mover.copy("sib", v, v, sib)

    def last(self):
        for h in (0, 1):
            self.mover.wait((h, 3))
            self.share(h, 3)

    def done(self):
        self.mover.wait("sib")


class Scatter:
    def __init__(self, g, at, mover, part, rows, out, cut, orders, bufs):
        self.g, self.at, self.mover, self.part, self.out, self.rows = g, at, mover, part, out, rows
        self.halves = halves(rows, part.shape[-1], cut)
        self.orders = orders
        self.sib, self.bufs = bufs[0], (bufs[1:4], bufs[4:7])

    def view(self, h, index):
        rows, lanes = self.halves[h]
        return self.part.at[index["z"], index["y"], index["x"], self.at["c"], rows, lanes]

    def index(self, h, stage, other=None):
        at, order = self.at, self.orders[h]
        index = {d: at[d] if d in order[:stage] else slice(None) for d in "zyx"}
        if other is not None:
            index[order[stage - 1]] = other
        return index

    def start(self):
        g, at = self.g, self.at
        src = self.part.at[:, :, :, 1 - at["c"], pl.ds(0, self.rows)]
        self.mover.copy("sib", src, self.sib, g.dev(g.sibling(at)))

    def send(self, stage):
        g, at = self.g, self.at
        if stage == 1:
            self.mover.wait("sib")
            rows, c = pl.ds(0, self.rows), at["c"]

            def add(i, carry):
                iz, iy, ix = i // (g.Y * g.X), (i // g.X) % g.Y, i % g.X
                self.part[iz, iy, ix, c, rows] = self.part[iz, iy, ix, c, rows] + self.sib[iz, iy, ix]
                return carry

            lax.fori_loop(0, g.Z * g.Y * g.X, add, 0)
        for h in (0, 1):
            if stage > 1:
                self.add(h, stage - 1)
            d = self.orders[h][stage - 1]
            for k in range(1, g.size[d]):
                to = g.moved(at, d, k)
                self.mover.copy((h, stage), self.view(h, self.index(h, stage, to[d])), self.bufs[h][stage - 1].at[k - 1], g.dev(to))

    def add(self, h, stage):
        g = self.g
        self.mover.wait((h, stage))
        free = [d for d in "zyx" if d not in self.orders[h][:stage]]
        sizes = [g.size[d] for d in free]
        buf = self.bufs[h][stage - 1]
        rows, lanes = self.halves[h]

        def body(i, carry):
            index = dict(self.at)
            place = []
            for n, d in zip(reversed(sizes), reversed(free)):
                index[d] = i % n
                place.insert(0, i % n)
                i = i // n
            where = (index["z"], index["y"], index["x"], self.at["c"], rows, lanes)
            v = self.part[where].astype(jnp.float32)
            for k in range(buf.shape[0]):
                v = v + buf[(k, *place)].astype(jnp.float32)
            self.part[where] = v.astype(self.part.dtype)
            return carry

        lax.fori_loop(0, math.prod(sizes), body, 0)

    def last(self, sem=None):
        at = self.at
        for h in (0, 1):
            self.mover.wait((h, 3))
            rows, lanes = self.halves[h]
            v = self.part[at["z"], at["y"], at["x"], at["c"], rows, lanes].astype(jnp.float32)
            buf = self.bufs[h][2]
            for k in range(buf.shape[0]):
                v = v + buf[k].astype(jnp.float32)
            self.out[rows, lanes] = v


def scatter_copies(g):
    return 1 + 2 * sum(n - 1 for n in g.size.values())


def scatter_buffers(g, r, C, cut, orders, dtype):
    shapes = [(g.Z, g.Y, g.X, r, C)]
    for hs, order in zip(half_shapes(r, C, cut), orders):
        for stage in (1, 2, 3):
            free = [g.size[d] for d in "zyx" if d not in order[:stage]]
            shapes.append((g.size[order[stage - 1]] - 1, *free, *hs))
    return [pltpu.VMEM(s, dtype) for s in shapes]


ZXY, XZY = (("z", "x", "y"), ("z", "y", "x")), (("x", "z", "y"), ("y", "z", "x"))
YXZ, YZX = (("y", "x", "z"), ("x", "y", "z")), (("y", "z", "x"), ("x", "z", "y"))


bf16, f32 = jnp.bfloat16, jnp.float32


def dot_nn(left, right):
    return jnp.dot(left, right, preferred_element_type=f32)


def dot_nt(left, right):
    return lax.dot_general(left, right, (((1,), (1,)), ((), ())), preferred_element_type=f32)


def dot_tn(left, right):
    return lax.dot_general(left, right, (((0,), (0,)), ((), ())), preferred_element_type=f32)


def block(i, n):
    return pl.ds(pl.multiple_of(i * n, n), n)


def normalize(v):
    width = v.shape[1]
    center = v - jnp.sum(v, axis=1, keepdims=True) * (1.0 / width)
    spread = jnp.sum(center * center, axis=1, keepdims=True) * (1.0 / width)
    scale = lax.rsqrt(spread + 1e-05)
    return center * scale, scale


def norm_forward(src, gain, dst):
    def body(i, carry):
        rows = block(i, 64)
        n, _ = normalize(src[rows, :])
        dst[rows, :] = (n * gain).astype(bf16)
        return carry

    lax.fori_loop(0, src.shape[0] // 64, body, 0)


def norm_backward(src, gain, up, put):
    width = src.shape[1]

    def body(i, total):
        rows = block(i, 64)
        n, scale = normalize(src[rows, :])
        u = up[rows, :]
        a = u * gain
        mean_a = jnp.sum(a, axis=1, keepdims=True) * (1.0 / width)
        mean_an = jnp.sum(a * n, axis=1, keepdims=True) * (1.0 / width)
        put(rows, scale * (a - mean_a - n * mean_an))
        return total + jnp.sum((u * n).reshape(8, 8, width), axis=0)

    return lax.fori_loop(0, src.shape[0] // 64, body, jnp.zeros((8, width), f32))


def places(g):
    return [(z, y, x, c) for z in range(g.Z) for y in range(g.Y) for x in range(g.X) for c in (0, 1)]


def layer_kernel(g, tensors, *refs):
    n_in, n_out = 14, 9
    (table_s, up_s, time_s, qkv_s, out_s, in_s, down_s, one_s, two_s, ids, steps, segs, noise, cot) = refs[:n_in]
    (output, noise_grad, table_o, small_o, qkv_o, out_o, in_o, down_o, gains_o) = refs[n_in : n_in + n_out]
    rest = list(refs[n_in + n_out :])
    take = lambda n: [rest.pop(0) for _ in range(n)]
    (small_s, gains_s, wtable, wsmall, wgains, wqkv, wout, win, wdown) = take(9)
    (small_nat, qkv_nat, out_nat, gain_rows, factor_s, level_s) = take(6)
    (feats, emb, normed, mixed, context, lse, mid, normed_two, act, slope, grad_t, raw, bias) = take(13)
    bufs = {name: take(7) for name in ("down", "in", "out", "qkv", "small", "gains", "table")}
    local, ag_send, ag_recv, rs_send, rs_recv = take(5)

    at = g.here()
    tokens, width = cot.shape
    rows = up_s.shape[0]
    heads = width // HEAD_DIM
    vocab = table_s.shape[0] * g.Z * g.F
    hidden = in_s.shape[0] * g.Z * g.F
    groups = tokens // 64
    spots = places(g)

    small_s[:, :EMBED] = up_s[...]
    small_s[:, EMBED:] = time_s[...]
    gains_s[...] = jnp.zeros_like(gains_s)
    gains_s[0:1, 0:rows] = one_s[...].astype(f32)
    gains_s[8:9, 0:rows] = two_s[...].astype(f32)
    tv = table_s[...].astype(f32)
    norms = jnp.sqrt(jnp.sum(tv * tv, axis=1, keepdims=True) + 1e-06)
    gains_s[9:10, :] = jnp.broadcast_to(jnp.sum(norms, axis=0, keepdims=True), (1, 128))

    enter(g, at)
    shards = {"gains": gains_s, "small": small_s, "table": table_s, "qkv": qkv_s, "out": out_s, "in": in_s, "down": down_s}
    fulls = {"gains": wgains, "small": wsmall, "table": wtable, "qkv": wqkv, "out": wout, "in": win, "down": wdown}
    ag = {}
    for i, name in enumerate(shards):
        cut, orders, _ = tensors[name]
        ag[name] = Gather(g, at, Mover(ag_send.at[i], ag_recv.at[i]), shards[name], fulls[name], cut, orders)
        ag[name].own(local.at[i])
        ag[name].send(1)
    first = [ag["gains"], ag["small"], ag["table"]]

    is_long = segs[tokens - 1] == 0
    row_block = lax.broadcasted_iota(jnp.int32, (tokens, tokens), 0) // 64
    col_block = lax.broadcasted_iota(jnp.int32, (tokens, tokens), 1) // 64
    bias[...] = jnp.where(row_block == col_block, 0.0, jnp.where(is_long, 0.0, -1e30)).astype(bf16)
    sub = lax.broadcasted_iota(jnp.int32, (8, 128), 0)
    lane = lax.broadcasted_iota(jnp.int32, (8, 128), 1)
    t = jnp.zeros((8, 128), f32)
    for i in range(groups):
        t = jnp.where(sub == i, steps[64 * i].astype(f32), t)
    level = t / STEPS + 0.0001
    level_s[0:8, :] = jnp.sqrt(1.0 - jnp.sqrt(level))
    level_s[8:16, :] = jnp.sqrt(jnp.sqrt(level))
    half = TIME_DIM // 2
    angles = t * jnp.exp(-math.log(10000.0) * (lane % half).astype(f32) / half)
    waves = jnp.where(lane < half, jnp.sin(angles), jnp.cos(angles))
    for i in range(groups):
        feats[64 * i : 64 * i + 64, EMBED:] = jnp.broadcast_to(waves[i : i + 1], (64, TIME_DIM)).astype(bf16)
    ids_row = ids[...].astype(f32)
    ids_col = jnp.transpose(jnp.broadcast_to(ids_row, (128, tokens)))

    for s in first:
        s.send(2)
    for s in first:
        s.send(3)
    ag["qkv"].send(2)
    for s in first:
        s.last()
    ag["out"].send(2)
    for s in first:
        s.done()

    ones = [jnp.zeros((8, 128), f32) for _ in range(width // 128)]
    twos = [jnp.zeros((8, 128), f32) for _ in range(width // 128)]
    total = jnp.zeros((8, 128), f32)
    for d, spot in enumerate(spots):
        a, b = wgains[(*spot, pl.ds(0, 8))], wgains[(*spot, pl.ds(8, 8))]
        total = total + b
        j, shift = (rows * d) // 128, (rows * d) % 128
        for acc, v in ((ones, a), (twos, b)):
            v = jnp.where(sub == 0, v, 0.0)
            r = pltpu.roll(v, shift, axis=1) if shift else v
            if shift + rows <= 128:
                acc[j] = acc[j] + r
            else:
                acc[j] = acc[j] + jnp.where(lane >= shift, r, 0.0)
                acc[j + 1] = acc[j + 1] + jnp.where(lane < shift, r, 0.0)
    for j in range(width // 128):
        gain_rows[0:8, 128 * j : 128 * j + 128] = ones[j]
        gain_rows[8:16, 128 * j : 128 * j + 128] = twos[j]
    factor = math.sqrt(EMBED) / (jnp.broadcast_to(total[1:2, :], (8, 128)) * (1.0 / vocab))
    factor_s[...] = factor
    for d, spot in enumerate(spots):
        small_nat[rows * d : rows * d + rows, :] = wsmall[spot]

    table = wtable.reshape(vocab, EMBED)
    span = 1024
    raw[...] = jnp.zeros_like(raw)

    def pick(i, carry):
        base = (i * span).astype(f32)
        cells = [
            jnp.where(ids_col == (lax.broadcasted_iota(jnp.int32, (tokens, 128), 1) + 128 * b).astype(f32) + base, 1.0, 0.0).astype(bf16)
            for b in range(span // 128)
        ]
        raw[...] += dot_nn(jnp.concatenate(cells, axis=1), table[block(i, span), :])
        return carry

    lax.fori_loop(0, vocab // span, pick, 0)
    ag["qkv"].send(3)
    for i in range(groups):
        r = slice(64 * i, 64 * i + 64)
        signal, blur = level_s[i : i + 1, :], level_s[8 + i : 9 + i, :]
        feats[r, :EMBED] = (signal * (raw[r, :] * factor_s[0:1, :]) + blur * noise[r, :].astype(f32)).astype(bf16)
    emb[...] = dot_nt(feats[...], small_nat[...])
    norm_forward(emb, gain_rows[0:1, :], normed)
    ag["out"].send(3)
    ag["in"].send(2)
    ag["qkv"].last()
    ag["qkv"].done()

    for d, spot in enumerate(spots):
        qkv_nat[3 * rows * d : 3 * rows * (d + 1), :] = wqkv[(*spot, pl.ds(0, 3 * rows))]

    def project(j, carry):
        mixed[:, block(j, width)] = dot_nt(normed[...], qkv_nat[block(j, width), :]).astype(bf16)
        return carry

    lax.fori_loop(0, 3, project, 0)
    ag["out"].last()

    lane_head = lax.broadcasted_iota(jnp.int32, (tokens, 128), 1) // HEAD_DIM
    sub_head = lax.broadcasted_iota(jnp.int32, (128, tokens), 0) // HEAD_DIM
    zero = jnp.zeros((), bf16)
    span_q = 256
    scale = 1.0 / math.sqrt(HEAD_DIM)

    def attend(p, carry):
        q = mixed[:, block(p, 128)] * jnp.asarray(scale, bf16)
        k = mixed[:, pl.ds(pl.multiple_of(width + p * 128, 128), 128)]
        v = mixed[:, pl.ds(pl.multiple_of(2 * width + p * 128, 128), 128)]
        vt = jnp.transpose(v)
        for c in range(0, tokens, span_q):
            ct = jnp.zeros((128, span_q), f32)
            for h in (0, 1):
                s = dot_nt(k, jnp.where(lane_head == h, q, zero)[c : c + span_q]) + bias[:, c : c + span_q].astype(f32)
                peak = jnp.max(s, axis=0, keepdims=True)
                e = jnp.exp(s - peak)
                total = jnp.sum(e, axis=0, keepdims=True)
                lse[pl.ds(2 * p + h, 1), c : c + span_q] = peak + jnp.log(total)
                probs = (e * (1.0 / total)).astype(bf16)
                ct = ct + dot_nn(jnp.where(sub_head == h, vt, zero), probs)
            context[c : c + span_q, block(p, 128)] = jnp.transpose(ct).astype(bf16)
        return carry

    pairs = heads // 2
    lax.fori_loop(0, pairs // 2, attend, 0)
    ag["in"].send(3)
    lax.fori_loop(pairs // 2, pairs, attend, 0)
    ag["down"].send(2)
    ag["out"].done()

    for d, spot in enumerate(spots):
        out_nat[rows * d : rows * d + rows, :] = wout[spot]
    mid[...] = emb[...] + dot_nt(context[...], out_nat[...])
    norm_forward(mid, gain_rows[8:9, :], normed_two)
    ag["in"].last()
    ag["down"].send(3)
    ag["in"].done()

    into = win.reshape(hidden, width)
    down = wdown.reshape(hidden, width)
    tile = 512

    def expand(j, carry):
        c = block(j, tile)
        pre = dot_nt(normed_two[...], into[c, :])
        phi = 0.5 * lax.erf(pre * math.sqrt(0.5)) + 0.5
        act[:, c] = (pre * phi).astype(bf16)
        slope[:, c] = (phi + pre * (jnp.exp(pre * pre * -0.5) * (1.0 / math.sqrt(2.0 * math.pi)))).astype(bf16)
        return carry

    lax.fori_loop(0, hidden // tile, expand, 0)
    ag["qkv"].mover.sent()
    grad_down = wqkv.reshape(hidden, width)

    def down_gradient(j, carry):
        c = block(j, tile)
        grad_down[c, :] = dot_tn(act[:, c], cot[...]).astype(bf16)
        return carry

    lax.fori_loop(0, hidden // tile, down_gradient, 0)

    rs = {}
    outs = {"down": down_o, "in": in_o, "out": out_o, "qkv": qkv_o, "small": small_o, "gains": gains_o, "table": table_o}
    parts = {"down": wqkv, "in": wdown, "out": wout, "qkv": win, "small": wsmall, "gains": wgains, "table": wtable}
    for i, name in enumerate(outs):
        cut, _, orders = tensors[name]
        rs[name] = Scatter(
            g, at, Mover(rs_send.at[i], rs_recv.at[i]), parts[name], outs[name].shape[0], outs[name], cut, orders, bufs[name]
        )
    rs["down"].start()
    ag["down"].last()
    rs["down"].send(1)
    ag["down"].done()

    output[...] = (mid[...] + dot_nn(act[...], down[...])).astype(bf16)

    def act_gradient(j, carry):
        c = block(j, tile)
        slope[:, c] = (dot_nt(cot[...], down[c, :]) * slope[:, c].astype(f32)).astype(bf16)
        return carry

    lax.fori_loop(0, hidden // tile, act_gradient, 0)
    ag["down"].mover.sent()

    def in_gradient(j, carry):
        c = block(j, tile)
        down[c, :] = dot_tn(slope[:, c], normed_two[...]).astype(bf16)
        return carry

    lax.fori_loop(0, hidden // tile, in_gradient, 0)
    rs["in"].start()
    rs["down"].send(2)
    grad_t[...] = dot_nn(slope[...], into[...])
    rs["in"].send(1)
    branch, grad_context, grad_emb = pl.ds(0, width), pl.ds(width, width), pl.ds(2 * width, width)

    def put_mid(r, grad):
        total = cot[r, :].astype(f32) + grad
        mid[r, :] = total
        act[r, branch] = total.astype(bf16)

    two_grad = norm_backward(mid, gain_rows[8:9, :], grad_t, put_mid)
    for s in ("gains", "small", "table", "out", "in"):
        ag[s].mover.sent()
    for j in range(2):
        part = dot_tn(act[:, pl.ds(j * width // 2, width // 2)], context[...])
        for d in range(len(spots) // 2):
            wout[spots[j * len(spots) // 2 + d]] = part[rows * d : rows * d + rows].astype(bf16)
    rs["out"].start()
    act[:, grad_context] = dot_nn(act[:, branch], out_nat[...]).astype(bf16)
    rs["out"].send(1)

    def attend_back(p, carry):
        q = mixed[:, block(p, 128)] * jnp.asarray(scale, bf16)
        k = mixed[:, pl.ds(pl.multiple_of(width + p * 128, 128), 128)]
        v = mixed[:, pl.ds(pl.multiple_of(2 * width + p * 128, 128), 128)]
        gc = act[:, pl.ds(pl.multiple_of(width + p * 128, 128), 128)]
        kt = jnp.transpose(k)
        gv = jnp.zeros((tokens, 128), f32)
        gk = jnp.zeros((tokens, 128), f32)
        for c in range(0, tokens, span_q):
            gq = jnp.zeros((128, span_q), f32)
            for h in (0, 1):
                qh = jnp.where(lane_head == h, q, zero)[c : c + span_q]
                gh = jnp.where(lane_head == h, gc, zero)[c : c + span_q]
                s = dot_nt(k, qh) + bias[:, c : c + span_q].astype(f32)
                probs = jnp.exp(s - lse[pl.ds(2 * p + h, 1), c : c + span_q])
                gv = gv + dot_nn(probs.astype(bf16), gh)
                weighed = probs * dot_nt(v, gh)
                gs = (weighed - probs * jnp.sum(weighed, axis=0, keepdims=True)).astype(bf16)
                gk = gk + dot_nn(gs, qh)
                gq = gq + dot_nn(jnp.where(sub_head == h, kt, zero), gs)
            mixed[c : c + span_q, block(p, 128)] = jnp.transpose(gq * scale).astype(bf16)
        mixed[:, pl.ds(pl.multiple_of(width + p * 128, 128), 128)] = gk.astype(bf16)
        mixed[:, pl.ds(pl.multiple_of(2 * width + p * 128, 128), 128)] = gv.astype(bf16)
        return carry

    lax.fori_loop(0, pairs // 2, attend_back, 0)
    rs["down"].send(3)
    rs["in"].send(2)
    lax.fori_loop(pairs // 2, pairs, attend_back, 0)
    rs["in"].send(3)
    rs["out"].send(2)

    grad_t[...] = dot_nn(mixed[...], qkv_nat[...])

    def qkv_gradient(j, carry):
        c = block(j, width // 2)
        qkv_nat[c, :] = dot_tn(mixed[:, c], normed[...]).astype(bf16)
        return carry

    lax.fori_loop(0, 6, qkv_gradient, 0)
    for d, spot in enumerate(spots):
        win[(*spot, pl.ds(0, 3 * rows))] = qkv_nat[3 * rows * d : 3 * rows * (d + 1), :]
    rs["qkv"].start()
    rs["out"].send(3)

    def put_emb(r, grad):
        act[r, grad_emb] = (mid[r, :] + grad).astype(bf16)

    one_grad = norm_backward(emb, gain_rows[0:1, :], grad_t, put_emb)
    rs["qkv"].send(1)
    part = dot_tn(act[:, grad_emb], feats[...])
    for d, spot in enumerate(spots):
        wsmall[spot] = part[rows * d : rows * d + rows].astype(bf16)
    rs["small"].start()
    one_grad = jnp.broadcast_to(jnp.sum(one_grad, axis=0, keepdims=True), (8, width))
    two_grad = jnp.broadcast_to(jnp.sum(two_grad, axis=0, keepdims=True), (8, width))
    for d, spot in enumerate(spots):
        j, shift = (rows * d) // 128, (rows * d) % 128
        for i, v in enumerate((one_grad, two_grad)):
            r = v[:, 128 * j : 128 * j + 128]
            if shift:
                r = pltpu.roll(r, 128 - shift, axis=1)
            if shift + rows > 128:
                r = jnp.where(lane < 128 - shift, r, pltpu.roll(v[:, 128 * j + 128 : 128 * j + 256], 128 - shift, axis=1))
            wgains[(*spot, pl.ds(8 * i, 8))] = r
    rs["gains"].start()
    raw[...] = dot_nn(act[:, grad_emb], small_nat[:, :EMBED])
    for i in range(groups):
        r = slice(64 * i, 64 * i + 64)
        grad = raw[r, :]
        noise_grad[r, :] = level_s[8 + i : 9 + i, :] * grad
        raw[r, :] = level_s[i : i + 1, :] * grad
    grad_rows = raw[...].astype(bf16)
    ids_all = jnp.broadcast_to(ids_row, (span, tokens))

    def count(i, carry):
        at_row = (lax.broadcasted_iota(jnp.int32, (span, tokens), 0) + i * span).astype(f32)
        table[block(i, span), :] = dot_nn(jnp.where(ids_all == at_row, 1.0, 0.0).astype(bf16), grad_rows).astype(bf16)
        return carry

    lax.fori_loop(0, vocab // span, count, 0)
    rs["table"].start()
    rs["small"].send(1)
    rs["gains"].send(1)
    rs["qkv"].send(2)
    rs["table"].send(1)
    rs["down"].last()
    rs["in"].last()
    rs["out"].last()
    rs["small"].send(2)
    rs["gains"].send(2)
    rs["qkv"].send(3)
    rs["table"].send(2)
    rs["small"].send(3)
    rs["gains"].send(3)
    rs["table"].send(3)
    for name in ("qkv", "small", "gains", "table"):
        rs[name].last()
    table_o[...] = table_o[...] * factor_s[0:1, :]
    for name in rs:
        rs[name].mover.sent()


def ring_local(
    g,
    embed_table,
    token_ids,
    time_steps,
    segment_ids,
    noise_draw,
    w_up,
    w_time,
    w_qkv,
    w_out,
    w_in,
    w_down,
    gain_one,
    gain_two,
    cotangent,
):
    tokens, width = cotangent.shape
    rows = w_up.shape[1]
    vocab_rows = embed_table.shape[0]
    hidden_rows = w_down.shape[0]
    lanes = ("lane", width // 2)
    tensors = {
        "gains": (("row", 8), ZXY, YXZ),
        "small": (("lane", EMBED), ZXY, YXZ),
        "table": (("row", vocab_rows // 2), ZXY, YXZ),
        "qkv": (lanes, ZXY, YXZ),
        "out": (lanes, ZXY, YXZ),
        "in": (lanes, ZXY, YXZ),
        "down": (lanes, XZY, YXZ),
    }
    shapes = {
        "down": (hidden_rows, width, bf16),
        "in": (hidden_rows, width, bf16),
        "out": (rows, width, bf16),
        "qkv": (3 * rows, width, bf16),
        "small": (rows, 2 * EMBED, bf16),
        "gains": (16, 128, f32),
        "table": (vocab_rows, EMBED, bf16),
    }
    lead = (g.Z, g.Y, g.X, 2)
    devices = g.Z * g.F
    hidden = hidden_rows * devices
    scratch = [
        pltpu.VMEM((rows, 2 * EMBED), bf16),
        pltpu.VMEM((16, 128), f32),
        pltpu.VMEM((*lead, vocab_rows, EMBED), bf16),
        pltpu.VMEM((*lead, rows, 2 * EMBED), bf16),
        pltpu.VMEM((*lead, 16, 128), f32),
        pltpu.VMEM((*lead, hidden_rows, width), bf16),
        pltpu.VMEM((*lead, rows, width), bf16),
        pltpu.VMEM((*lead, hidden_rows, width), bf16),
        pltpu.VMEM((*lead, hidden_rows, width), bf16),
        pltpu.VMEM((width, 2 * EMBED), bf16),
        pltpu.VMEM((3 * width, width), bf16),
        pltpu.VMEM((width, width), bf16),
        pltpu.VMEM((16, width), f32),
        pltpu.VMEM((8, 128), f32),
        pltpu.VMEM((16, 128), f32),
        pltpu.VMEM((tokens, 2 * EMBED), bf16),
        pltpu.VMEM((tokens, width), f32),
        pltpu.VMEM((tokens, width), bf16),
        pltpu.VMEM((tokens, 3 * width), bf16),
        pltpu.VMEM((tokens, width), bf16),
        pltpu.VMEM((16, tokens), f32),
        pltpu.VMEM((tokens, width), f32),
        pltpu.VMEM((tokens, width), bf16),
        pltpu.VMEM((tokens, hidden), bf16),
        pltpu.VMEM((tokens, hidden), bf16),
        pltpu.VMEM((tokens, width), f32),
        pltpu.VMEM((tokens, EMBED), f32),
        pltpu.VMEM((tokens, tokens), bf16),
    ]
    for name, (r, c, dtype) in shapes.items():
        cut, _, orders = tensors[name]
        scratch += scatter_buffers(g, r, c, cut, orders, dtype)
    n = len(shapes)
    scratch += [pltpu.SemaphoreType.DMA((n,))]
    scratch += [pltpu.SemaphoreType.DMA((n, gather_copies(g)))] * 2
    scratch += [pltpu.SemaphoreType.DMA((n, scatter_copies(g)))] * 2
    vm, sm = pl.BlockSpec(memory_space=pltpu.VMEM), pl.BlockSpec(memory_space=pltpu.SMEM)
    shard = lambda name: jax.ShapeDtypeStruct(shapes[name][:2], f32)
    outs = pl.pallas_call(
        functools.partial(layer_kernel, g, tensors),
        out_shape=(
            jax.ShapeDtypeStruct((tokens, width), bf16),
            jax.ShapeDtypeStruct((tokens, EMBED), f32),
            *[shard(name) for name in ("table", "small", "qkv", "out", "in", "down", "gains")],
        ),
        in_specs=[vm] * 10 + [sm] * 2 + [vm] * 2,
        out_specs=(vm,) * 9,
        scratch_shapes=scratch,
        compiler_params=pltpu.CompilerParams(
            collective_id=0, has_side_effects=True, vmem_limit_bytes=67043328
        ),
        name="layer",
    )(
        embed_table,
        w_up.T,
        w_time.T,
        w_qkv.T,
        w_out.T,
        w_in.T,
        w_down,
        gain_one.reshape(1, rows),
        gain_two.reshape(1, rows),
        token_ids.reshape(1, tokens),
        time_steps,
        segment_ids,
        noise_draw,
        cotangent,
    )
    output, noise_grad, table_own, small_own, qkv_own, out_own, in_own, down_own, gains_own = outs
    return (
        output,
        table_own,
        noise_grad,
        small_own[:, :EMBED].T,
        small_own[:, EMBED:].T,
        qkv_own.T,
        out_own.T,
        in_own.T,
        down_own,
        gains_own[0, :rows],
        gains_own[8, :rows],
    )


def solution(mesh):
    in_specs = (
        P(("dp", "fsdp"), None),
        P(("dp", "fsdp")),
        P(("dp", "fsdp")),
        P(("dp", "fsdp")),
        P(("dp", "fsdp"), None),
        P(None, ("dp", "fsdp")),
        P(None, ("dp", "fsdp")),
        P(None, ("dp", "fsdp")),
        P(None, ("dp", "fsdp")),
        P(None, ("dp", "fsdp")),
        P(("dp", "fsdp"), None),
        P(("dp", "fsdp")),
        P(("dp", "fsdp")),
        P(("dp", "fsdp"), None),
    )
    out_specs = (
        P(("dp", "fsdp"), None),
        P(("dp", "fsdp"), None),
        P(("dp", "fsdp"), None),
        P(None, ("dp", "fsdp")),
        P(None, ("dp", "fsdp")),
        P(None, ("dp", "fsdp")),
        P(None, ("dp", "fsdp")),
        P(None, ("dp", "fsdp")),
        P(("dp", "fsdp"), None),
        P(("dp", "fsdp")),
        P(("dp", "fsdp")),
    )
    grid = Grid(mesh.shape["dp"], mesh.shape["fsdp"])

    def local(*args):
        if all(rows % 8 == 0 for rows in (args[5].shape[1], args[10].shape[0])):
            return ring_local(grid, *args)
        return native_local(*args)

    return jax.shard_map(local, mesh=mesh, in_specs=in_specs, out_specs=out_specs, check_vma=False)
```
